32 devices in a mesh: groups: 2 (over y), space: 16 (over z, x, core).
Axes of the slice: x: 2, y: 2, z: 4, core: 2. Of those that a mesh axis runs over, the one named last changes fastest.
Arguments:
- modes: float32 [4, 128, 32, 64], P('groups', None, 'space'), parts along dimension 0, may hold values from -6 to 6
- cell_weight: float32 [32, 128], P('space', 'groups'), parts along dimension 1, may hold values from 0.5 to 2
- seeds: int32 [256], P(('groups', 'space')), parts along dimension 0, may hold values from 0 to 255
- coeff_table: float32 [256, 128], replicated, may hold values from -6 to 6
- force_table: float32 [256, 128], replicated, may hold values from -6 to 6
- visc_table: float32 [256], replicated, may hold values from 0.02 to 0.2
Outputs:
- coefficients: float32 [256, 128], P(('groups', 'space')), parts along dimension 0
The draws below stay inside these ranges and needn't reach their ends.
There are 2 independent parts, one for each index of `groups`. The reference program is written for one: setup_inputs(seed, part) draws one part's arguments, and reference() takes and returns one part's arrays. A program takes and returns all parts, laid end to end along the dimension named above; an argument that names none is the same for every part. Nothing has to cross between parts.
All inputs are finite; a program needn't handle non-finite values.
Results may differ from the reference program's by a relative error of at most 0.00013.
Values sent between devices are 32-bit elements; how exact they have to be, the bound alone decides.
A program may use at most 64 MiB of HBM per device.

```python
import math
import jax
import jax.numpy as jnp
from jax import lax

M = 128
NY = 64
PARAMS = 256
STEPS = 2
NX = 32
TRAJ = 128


def plant(drawn, rng, low, top_value):
    longest = drawn.shape.index(max(drawn.shape))
    spots = []
    for shift in (0, 1):
        where = [jax.random.randint(jax.random.fold_in(rng, axis), (), 0, length) for axis, length in enumerate(drawn.shape)]
        where[longest] = (where[longest] + shift) % drawn.shape[longest]
        spots.append(tuple(where))
    return drawn.at[spots[0]].set(low).at[spots[1]].set(top_value)


def block_scale(stream_key, extent, shards, smallest, top_value):
    factor_of = 1.0
    for axis_at, parts in shards:
        steps = jax.random.uniform(jax.random.fold_in(jax.random.fold_in(stream_key, 6), axis_at), (parts,), jnp.float32, smallest / len(shards), top_value / len(shards))
        factor_of = factor_of * jnp.repeat(jnp.exp(steps), extent[axis_at] // parts).reshape((-1,) + (1,) * (len(extent) - 1 - axis_at))
    return factor_of


def scatter_about(stream_key, extent, deviation, reach, shards=(), held_as=jnp.bfloat16):
    values = deviation * jax.random.normal(stream_key, extent, jnp.float32)
    if shards:
        values = values * block_scale(stream_key, extent, shards, -0.22, 0.18)
    return jnp.clip(values, -reach, reach).astype(held_as)


def setup_inputs(seed: int = 0, part: int = 0) -> dict:
    streams_of = jax.random.split(jax.random.key(seed), 7)
    part_keys = jax.random.split(jax.random.fold_in(streams_of[6], part), 7)
    return {
        "modes": scatter_about(part_keys[0], (2, M, NX, NY), 1.0, 6.0, ((2, 16),), jnp.float32),
        "cell_weight": jnp.clip(jnp.exp(math.log(2.0) - 1.3862944 * jax.random.uniform(part_keys[1], (NX, NY), jnp.float32) ** block_scale(part_keys[1], (NX, NY), ((0, 16),), -0.2, 0.2)), 0.5, 2.0),
        "seeds": plant(jax.random.randint(part_keys[2], (TRAJ,), 0, PARAMS), jax.random.fold_in(part_keys[2], 1), 0, PARAMS - 1).astype(jnp.int32),
        "coeff_table": scatter_about(streams_of[3], (PARAMS, M), 1.0, 6.0, (), jnp.float32),
        "force_table": scatter_about(streams_of[4], (PARAMS, M), 1.0, 6.0, (), jnp.float32),
        "visc_table": jnp.clip(jnp.exp(jax.random.uniform(streams_of[5], (PARAMS,), jnp.float32, math.log(0.02), math.log(0.2))), 0.02, 0.2),
    }


TIME_STEP = 0.5


def slopes_of(modes):
    along = (jnp.roll(modes, 2, 2) - 8.0 * jnp.roll(modes, 1, 2) + 8.0 * jnp.roll(modes, -1, 2) - jnp.roll(modes, -2, 2)) / 12.0
    across = (jnp.roll(modes, 2, 3) - 8.0 * jnp.roll(modes, 1, 3) + 8.0 * jnp.roll(modes, -1, 3) - jnp.roll(modes, -2, 3)) / 12.0
    return jnp.stack([along, across])


def reference(modes, cell_weight, seeds, coeff_table, force_table, visc_table):
    cell_count = NX * NY
    slopes = slopes_of(modes).reshape(2, 2, M, cell_count)
    velocity = modes.reshape(2, M, cell_count)
    cell_scale = cell_weight.reshape(cell_count) / cell_count
    weighted = velocity * cell_scale[None, None, :]
    diffusion = jnp.einsum("taic,tajc->ij", slopes * cell_scale[None, None, None, :], slopes, precision=lax.Precision.HIGHEST)
    block_size = 4

    def project(block_index):
        weighted_block = lax.dynamic_slice_in_dim(weighted, block_index * block_size, block_size, 1)
        advected = jnp.sum(weighted_block[None, :, :, None, :] * slopes[:, :, None, :, :], axis=1)
        return jnp.einsum("tjc,tikc->ijk", velocity, advected, precision=lax.Precision.HIGHEST)

    tensor = lax.map(project, jnp.arange(M // block_size, dtype=jnp.int32)).reshape(M * M, M)
    selector = (seeds[:, None] == jnp.arange(PARAMS, dtype=jnp.int32)[None, :]).astype(jnp.float32)
    coeffs = jnp.dot(selector, coeff_table, precision=lax.Precision.HIGHEST)
    forcing = jnp.dot(selector, force_table, precision=lax.Precision.HIGHEST)
    viscosity = jnp.dot(selector, visc_table, precision=lax.Precision.HIGHEST)
    for repeat in range(STEPS):
        paired = jnp.dot(coeffs, tensor.T, precision=lax.Precision.HIGHEST).reshape(TRAJ, M, M)
        quadratic = jnp.sum(paired * coeffs[:, None, :], axis=2)
        linear = jnp.dot(coeffs, diffusion, precision=lax.Precision.HIGHEST)
        coeffs = coeffs + TIME_STEP * (forcing - viscosity[:, None] * linear - quadratic)
    return coeffs
```

```python
import functools

import jax
import jax.numpy as jnp
from jax import lax
from jax.experimental import pallas as pl
from jax.experimental.pallas import tpu as pltpu
from jax.sharding import PartitionSpec as P

STEPS = 2


TIME_STEP = 0.5

WIDTH = 2

HIGHEST = lax.Precision.HIGHEST

MESH = pl.DeviceIdType.MESH


def dot(a, b, contract=((1,), (0,))):
    return lax.dot_general(
        a, b, (contract, ((), ())), precision=HIGHEST, preferred_element_type=jnp.float32
    )


def kernel(
    n,
    across,
    modes_ref,
    weight_ref,
    seeds_ref,
    visc_ref,
    coeff_ref,
    force_ref,
    out_ref,
    halo,
    seeds_all,
    basis,
    fields,
    coeffs,
    partial,
    landed,
    halo_send,
    halo_recv,
    send_sem,
    recv_sem,
):
    me = lax.axis_index("space")
    own = seeds_ref.shape[0]
    modes_n = modes_ref.shape[1]
    cells = modes_ref.shape[2]
    edge = WIDTH * across
    params = coeff_ref.shape[0]
    total = own * n
    own_rows = pl.ds(pl.multiple_of(me * own, own), own)

    barrier = pltpu.get_barrier_semaphore()

    @pl.loop(1, n)
    def _(d):
        pl.semaphore_signal(
            barrier, inc=1, device_id={"space": lax.rem(me + d, n)}, device_id_type=MESH
        )

    def lateral(x, shift):
        lane = lax.rem(lax.broadcasted_iota(jnp.int32, x.shape, 1), across)
        inside = pltpu.roll(x, shift % cells, 1)
        around = pltpu.roll(x, (shift + (-across if shift > 0 else across)) % cells, 1)
        crossed = lane < shift if shift > 0 else lane >= across + shift
        return jnp.where(crossed, around, inside)

    for a in range(2):
        f = modes_ref[a]
        basis[:, a * cells : (a + 1) * cells] = f
        q = 4 + a
        basis[:, q * cells : (q + 1) * cells] = (
            lateral(f, 2) - 8.0 * lateral(f, 1) + 8.0 * lateral(f, -1) - lateral(f, -2)
        ) / 12.0
    seeds_all[own_rows, :] = seeds_ref[...]

    def selector(seeds):
        return (
            seeds[:, 0:1]
            == lax.broadcasted_iota(jnp.int32, (seeds.shape[0], params), 1)
        ).astype(jnp.float32)

    mine = selector(seeds_ref[...])
    forcing = dot(mine, force_ref[...])
    own_coeffs = dot(mine, coeff_ref[...])

    pl.semaphore_wait(barrier, n - 1)

    def halo_copy(src, slot, peer):
        return pltpu.make_async_remote_copy(
            src_ref=src,
            dst_ref=halo.at[slot],
            send_sem=halo_send.at[slot],
            recv_sem=halo_recv.at[slot],
            device_id={"space": peer},
            device_id_type=MESH,
        )

    def spread(phase, source, target):
        @pl.loop(1, n)
        def _(d):
            peer = lax.rem(me + d, n)
            pltpu.make_async_remote_copy(
                src_ref=source(peer),
                dst_ref=target(d),
                send_sem=send_sem.at[phase],
                recv_sem=recv_sem.at[phase],
                device_id={"space": peer},
                device_id_type=MESH,
            ).start()

    def whole(phase, ref):
        return pltpu.make_async_remote_copy(
            src_ref=ref,
            dst_ref=ref,
            send_sem=send_sem.at[phase],
            recv_sem=recv_sem.at[phase],
            device_id={"space": lax.rem(me + 1, n)},
            device_id_type=MESH,
        )

    up = halo_copy(modes_ref.at[:, :, pl.ds(cells - edge, edge)], 0, lax.rem(me + 1, n))
    down = halo_copy(modes_ref.at[:, :, pl.ds(0, edge)], 1, lax.rem(me + n - 1, n))
    spread(0, lambda peer: seeds_ref, lambda d: seeds_all.at[own_rows, :])
    up.start()
    down.start()

    seed_bytes = whole(0, seeds_all.at[pl.ds(0, total - own), :])
    seed_bytes.wait_recv()
    select = selector(seeds_all[...])
    now = dot(select, coeff_ref[...])
    viscosity = jnp.sum(select * visc_ref[...], axis=1, keepdims=True)
    up.wait_recv()
    down.wait_recv()
    for a in range(2):
        padded = jnp.concatenate([halo[0, a], modes_ref[a], halo[1, a]], axis=1)
        span = cells + 2 * edge
        slope = (
            pltpu.roll(padded, 2 * across, 1)
            - 8.0 * pltpu.roll(padded, across, 1)
            + 8.0 * pltpu.roll(padded, span - across, 1)
            - pltpu.roll(padded, span - 2 * across, 1)
        ) / 12.0
        q = 2 + a
        basis[:, q * cells : (q + 1) * cells] = slope[:, edge : edge + cells]

    scale = weight_ref[...] / (cells * n)
    for step in range(STEPS):
        gathered = dot(now, basis[...])
        part = [gathered[:, q * cells : (q + 1) * cells] for q in range(6)]
        for a in range(2):
            fields[:, a * cells : (a + 1) * cells] = scale * (
                part[0] * part[2 + a] + part[1] * part[4 + a]
            )
        damped = viscosity * scale
        for q in range(2, 6):
            fields[:, q * cells : (q + 1) * cells] = damped * part[q]
        partial[step] = dot(fields[...], basis[...], ((1,), (1,)))
        spread(
            1 + 2 * step,
            lambda peer: partial.at[step, pl.ds(pl.multiple_of(peer * own, own), own), :],
            lambda d: landed.at[step, d - 1],
        )
        change = partial[step, own_rows, :]
        whole(1 + 2 * step, landed.at[step]).wait_recv()
        change = change + jnp.sum(landed[step], axis=0)
        own_coeffs = own_coeffs + TIME_STEP * (forcing - change)
        if step < STEPS - 1:
            coeffs[step, own_rows, :] = own_coeffs
            spread(
                2 + 2 * step,
                lambda peer: coeffs.at[step, own_rows, :],
                lambda d: coeffs.at[step, own_rows, :],
            )
            whole(2 + 2 * step, coeffs.at[step, pl.ds(0, total - own), :]).wait_recv()
            now = coeffs[step]
    out_ref[...] = own_coeffs

    up.wait_send()
    down.wait_send()
    seed_bytes.wait_send()
    for step in range(STEPS):
        whole(1 + 2 * step, landed.at[step]).wait_send()
        if step < STEPS - 1:
            whole(2 + 2 * step, coeffs.at[step, pl.ds(0, total - own), :]).wait_send()


def shards(modes, cell_weight, seeds, coeff_table, force_table, visc_table):
    components, mode_count, slab_cells, across = modes.shape
    n = lax.axis_size("space")
    cells = slab_cells * across
    own = seeds.shape[0]
    total = own * n
    vmem = pl.BlockSpec(memory_space=pltpu.VMEM)
    return pl.pallas_call(
        functools.partial(kernel, n, across),
        out_shape=jax.ShapeDtypeStruct((own, mode_count), jnp.float32),
        in_specs=[vmem] * 6,
        out_specs=vmem,
        scratch_shapes=[
            pltpu.VMEM((2, components, mode_count, WIDTH * across), jnp.float32),
            pltpu.VMEM((total, 128), jnp.int32),
            pltpu.VMEM((mode_count, 6 * cells), jnp.float32),
            pltpu.VMEM((total, 6 * cells), jnp.float32),
            pltpu.VMEM((STEPS - 1, total, mode_count), jnp.float32),
            pltpu.VMEM((STEPS, total, mode_count), jnp.float32),
            pltpu.VMEM((STEPS, n - 1, own, mode_count), jnp.float32),
            pltpu.SemaphoreType.DMA((2,)),
            pltpu.SemaphoreType.DMA((2,)),
            pltpu.SemaphoreType.DMA((2 * STEPS,)),
            pltpu.SemaphoreType.DMA((2 * STEPS,)),
        ],
        compiler_params=pltpu.CompilerParams(collective_id=0, has_side_effects=True),
    )(
        modes.reshape(components, mode_count, cells),
        cell_weight.reshape(1, cells),
        jnp.broadcast_to(seeds[:, None], (own, 128)),
        visc_table.reshape(1, -1),
        coeff_table,
        force_table,
    )


def solution(mesh):
    placed = (
        P("groups", None, "space", None),
        P("space", "groups"),
        P(("groups", "space")),
        P(),
        P(),
        P(),
    )
    return jax.shard_map(
        shards, mesh=mesh, in_specs=placed, out_specs=P(("groups", "space"), None), check_vma=False
    )
```

```python
import functools

import jax
import jax.numpy as jnp
from jax import lax
from jax.experimental import pallas as pl
from jax.experimental.pallas import tpu as pltpu
from jax.sharding import PartitionSpec as P

STEPS = 2


TIME_STEP = 0.5

MESH = pl.DeviceIdType.MESH

ROWS = ((1,), (0,))
LANES = ((1,), (1,))


def split(x):
    high = x.astype(jnp.bfloat16)
    return high, (x - high.astype(jnp.float32)).astype(jnp.bfloat16)


def product(a, b, contract):
    return lax.dot_general(a, b, (contract, ((), ())), preferred_element_type=jnp.float32)


def product_3(a, b, contract):
    return (
        product(a[0], b[1], contract) + product(a[1], b[0], contract)
    ) + product(a[0], b[0], contract)


def kernel(
    n,
    across,
    modes_hbm,
    weight_hbm,
    seeds_hbm,
    visc_hbm,
    coeff_hbm,
    force_hbm,
    out_ref,
    modes_ref,
    weight_ref,
    seeds_ref,
    visc_ref,
    coeff_ref,
    force_ref,
    seed_rows,
    high,
    low,
    coeffs,
    partial,
    landed,
    load_sem,
    halo_send,
    halo_recv,
    send_sem,
    recv_sem,
):
    me = lax.axis_index("space")
    own = seeds_hbm.shape[0]
    cells = modes_hbm.shape[1]
    slab = cells // across
    params = coeff_ref.shape[0]
    total = own * n
    own_rows = pl.ds(pl.multiple_of(me * own, own), own)
    before, after = lax.rem(me + n - 1, n), lax.rem(me + 1, n)

    barrier = pltpu.get_barrier_semaphore()

    @pl.loop(1, n)
    def _(d):
        pl.semaphore_signal(
            barrier, inc=1, device_id={"space": lax.rem(me + d, n)}, device_id_type=MESH
        )

    loads = [
        pltpu.make_async_copy(source, target, load_sem.at[i])
        for i, (source, target) in enumerate(
            (
                (seeds_hbm, seeds_ref),
                (modes_hbm, modes_ref.at[:, pl.ds(cells, cells), :]),
                (coeff_hbm, coeff_ref),
                (force_hbm, force_ref),
                (visc_hbm, visc_ref),
                (weight_hbm, weight_ref),
            )
        )
    ]
    for load in loads:
        load.start()
    loads[0].wait()
    lane = lax.broadcasted_iota(jnp.int32, (1, total), 1)
    row = jnp.zeros((1, total), jnp.int32)
    column = jnp.zeros((own, params), jnp.int32)
    for r in range(own):
        row = jnp.where(lane == me * own + r, seeds_ref[r], row)
        column = jnp.where(
            lax.broadcasted_iota(jnp.int32, (own, params), 0) == r, seeds_ref[r], column
        )
    seed_rows[0] = row
    loads[1].wait()

    pl.semaphore_wait(barrier, n - 1)

    def spread(phase, source, target):
        @pl.loop(1, n)
        def _(d):
            peer = lax.rem(me + d, n)
            pltpu.make_async_remote_copy(
                src_ref=source(peer),
                dst_ref=target(d),
                send_sem=send_sem.at[phase],
                recv_sem=recv_sem.at[phase],
                device_id={"space": peer},
                device_id_type=MESH,
            ).start()

    def whole(phase, ref):
        return pltpu.make_async_remote_copy(
            src_ref=ref,
            dst_ref=ref,
            send_sem=send_sem.at[phase],
            recv_sem=recv_sem.at[phase],
            device_id={"space": after},
            device_id_type=MESH,
        )

    def halo_copy(slot, place, peer):
        return pltpu.make_async_remote_copy(
            src_ref=modes_ref.at[:, pl.ds(cells, cells), :],
            dst_ref=modes_ref.at[:, pl.ds(place * cells, cells), :],
            send_sem=halo_send.at[slot],
            recv_sem=halo_recv.at[slot],
            device_id={"space": peer},
            device_id_type=MESH,
        )

    up = halo_copy(0, 0, after)
    down = halo_copy(1, 2, before)
    up.start()
    down.start()
    spread(0, lambda peer: seed_rows.at[0], lambda d: seed_rows.at[d])

    def keep(q, x):
        high[q * cells : (q + 1) * cells, :], low[q * cells : (q + 1) * cells, :] = split(x)

    def lateral(f, shift):
        layers = [
            pltpu.roll(f[s * across : (s + 1) * across], shift % across, 0) for s in range(slab)
        ]
        return jnp.concatenate(layers, axis=0)

    for a in range(2):
        f = modes_ref[a, cells : 2 * cells, :]
        keep(a, f)
        keep(
            4 + a,
            (lateral(f, 2) - 8.0 * lateral(f, 1) + 8.0 * lateral(f, -1) - lateral(f, -2)) / 12.0,
        )
    for load in loads[2:]:
        load.wait()
    mine = (column == lax.broadcasted_iota(jnp.int32, (own, params), 1)).astype(jnp.float32)
    forcing = lax.dot(mine, force_ref[...], precision=lax.Precision.HIGHEST)
    own_coeffs = lax.dot(mine, coeff_ref[...], precision=lax.Precision.HIGHEST)
    table = split(coeff_ref[...])
    scale = jnp.concatenate([weight_ref[s : s + 1, :] for s in range(slab)], axis=1) / (cells * n)

    seed_bytes = whole(0, seed_rows.at[pl.ds(1, n - 1)])
    seed_bytes.wait_recv()
    seeds = jnp.sum(seed_rows[...], axis=0)
    spot = jnp.broadcast_to(seeds.astype(jnp.float32), (128, total)).T
    spot = jnp.concatenate([spot] * (params // 128), axis=1)
    chosen = spot == lax.broadcasted_iota(jnp.int32, (total, params), 1).astype(jnp.float32)
    viscosity = jnp.sum(jnp.where(chosen, visc_ref[...], 0.0), axis=1, keepdims=True)
    chosen = chosen.astype(jnp.float32).astype(jnp.bfloat16)
    now = [product(chosen, half, ROWS).astype(jnp.bfloat16) for half in table]
    damped = viscosity * scale

    up.wait_recv()
    down.wait_recv()
    for a in range(2):
        f = [
            modes_ref[a, cells + shift * across : 2 * cells + shift * across, :]
            for shift in (-2, -1, 1, 2)
        ]
        keep(2 + a, (f[0] - 8.0 * f[1] + 8.0 * f[2] - f[3]) / 12.0)

    for step in range(STEPS):
        basis = (high[...], low[...])
        gathered = product_3(now, basis, LANES)
        part = [gathered[:, q * cells : (q + 1) * cells] for q in range(6)]
        fields = [scale * (part[0] * part[2 + a] + part[1] * part[4 + a]) for a in range(2)]
        fields += [damped * part[q] for q in range(2, 6)]
        partial[step] = product_3(split(jnp.concatenate(fields, axis=1)), basis, ROWS)
        spread(
            1 + 2 * step,
            lambda peer: partial.at[step, pl.ds(pl.multiple_of(peer * own, own), own), :],
            lambda d: landed.at[step, d - 1],
        )
        change = partial[step, own_rows, :]
        whole(1 + 2 * step, landed.at[step]).wait_recv()
        change = change + jnp.sum(landed[step], axis=0)
        own_coeffs = own_coeffs + TIME_STEP * (forcing - change)
        if step < STEPS - 1:
            coeffs[step, own_rows, :] = own_coeffs
            spread(
                2 + 2 * step,
                lambda peer: coeffs.at[step, own_rows, :],
                lambda d: coeffs.at[step, own_rows, :],
            )
            whole(2 + 2 * step, coeffs.at[step, pl.ds(0, total - own), :]).wait_recv()
            now = split(coeffs[step])
    out_ref[...] = own_coeffs

    up.wait_send()
    down.wait_send()
    seed_bytes.wait_send()
    for step in range(STEPS):
        whole(1 + 2 * step, landed.at[step]).wait_send()
        if step < STEPS - 1:
            whole(2 + 2 * step, coeffs.at[step, pl.ds(0, total - own), :]).wait_send()


def shards(modes, cell_weight, seeds, coeff_table, force_table, visc_table):
    components, mode_count, slab_cells, across = modes.shape
    n = lax.axis_size("space")
    cells = slab_cells * across
    own = seeds.shape[0]
    total = own * n
    params = coeff_table.shape[0]
    vmem = pl.BlockSpec(memory_space=pltpu.VMEM)
    return pl.pallas_call(
        functools.partial(kernel, n, across),
        out_shape=jax.ShapeDtypeStruct((own, mode_count), jnp.float32),
        in_specs=[pl.BlockSpec(memory_space=pl.ANY)] * 6,
        out_specs=vmem,
        scratch_shapes=[
            pltpu.VMEM((components, 3 * cells, mode_count), jnp.float32),
            pltpu.VMEM((slab_cells, across), jnp.float32),
            pltpu.SMEM((own,), jnp.int32),
            pltpu.VMEM((1, params), jnp.float32),
            pltpu.VMEM((params, mode_count), jnp.float32),
            pltpu.VMEM((params, mode_count), jnp.float32),
            pltpu.VMEM((n, 1, total), jnp.int32),
            pltpu.VMEM((6 * cells, mode_count), jnp.bfloat16),
            pltpu.VMEM((6 * cells, mode_count), jnp.bfloat16),
            pltpu.VMEM((STEPS - 1, total, mode_count), jnp.float32),
            pltpu.VMEM((STEPS, total, mode_count), jnp.float32),
            pltpu.VMEM((STEPS, n - 1, own, mode_count), jnp.float32),
            pltpu.SemaphoreType.DMA((6,)),
            pltpu.SemaphoreType.DMA((2,)),
            pltpu.SemaphoreType.DMA((2,)),
            pltpu.SemaphoreType.DMA((2 * STEPS,)),
            pltpu.SemaphoreType.DMA((2 * STEPS,)),
        ],
        compiler_params=pltpu.CompilerParams(collective_id=0, has_side_effects=True),
    )(
        modes.transpose(0, 2, 3, 1).reshape(components, cells, mode_count),
        cell_weight,
        seeds,
        visc_table.reshape(1, -1),
        coeff_table,
        force_table,
    )


def solution(mesh):
    placed = (
        P("groups", None, "space", None),
        P("space", "groups"),
        P(("groups", "space")),
        P(),
        P(),
        P(),
    )
    return jax.shard_map(
        shards, mesh=mesh, in_specs=placed, out_specs=P(("groups", "space"), None), check_vma=False
    )
```

```python
import functools

import jax
import jax.numpy as jnp
from jax import lax
from jax.experimental import pallas as pl
from jax.experimental.pallas import tpu as pltpu
from jax.sharding import PartitionSpec as P

TIME_STEP = 0.5

MESH = pl.DeviceIdType.MESH

ROWS = ((1,), (0,))
LANES = ((1,), (1,))


def split(x):
    high = x.astype(jnp.bfloat16)
    return high, (x - high.astype(jnp.float32)).astype(jnp.bfloat16)


def product(a, b, contract):
    return lax.dot_general(a, b, (contract, ((), ())), preferred_element_type=jnp.float32)


BLOCK = 4


def product_3(a, b, contract):
    rows = a[0].shape[0]
    both = product(jnp.concatenate(a, axis=0), b[0], contract)
    return (product(a[0], b[1], contract) + both[rows:]) + both[:rows]


def kernel(
    n,
    across,
    modes_hbm,
    weight_hbm,
    seeds_hbm,
    visc_hbm,
    coeff_hbm,
    force_hbm,
    out_ref,
    slabs,
    weights,
    seeds_ref,
    visc_ref,
    coeff_ref,
    force_ref,
    seed_rows,
    spots,
    high,
    low,
    wide_high,
    wide_low,
    partial,
    landed,
    group_sum,
    group_landed,
    group_coeffs,
    group_force,
    last,
    last_landed,
    load_sem,
    slab_send,
    slab_recv,
    send_sem,
    recv_sem,
):
    me = lax.axis_index("space")
    blocks = n // BLOCK
    block, seat = me // BLOCK, lax.rem(me, BLOCK)
    base = me - seat
    own = seeds_hbm.shape[0]
    cells = modes_hbm.shape[1]
    mode_count = modes_hbm.shape[2]
    slab = cells // across
    params = coeff_ref.shape[0]
    total = own * n
    group = own * blocks
    partner = me + 1 - 2 * lax.rem(seat, 2)
    mirror = base + BLOCK - 1 - seat
    place = seat + 1
    high_end = seat // (BLOCK - 1)
    outer = high_end * (BLOCK + 1)
    beyond = lax.rem(me + n - 1 + 2 * high_end, n)
    at_end = (seat == 0) | (seat == BLOCK - 1)
    inside = jnp.logical_not(at_end)

    barrier = pltpu.get_barrier_semaphore()

    @pl.loop(1, n)
    def _(d):
        pl.semaphore_signal(
            barrier, inc=1, device_id={"space": lax.rem(me + d, n)}, device_id_type=MESH
        )

    loads = [
        pltpu.make_async_copy(source, target, load_sem.at[i])
        for i, (source, target) in enumerate(
            (
                (seeds_hbm, seeds_ref),
                (modes_hbm, slabs.at[:, place]),
                (weight_hbm, weights.at[seat]),
                (coeff_hbm, coeff_ref),
                (force_hbm, force_ref),
                (visc_hbm, visc_ref),
            )
        )
    ]
    for load in loads:
        load.start()
    loads[0].wait()
    lane = lax.broadcasted_iota(jnp.int32, (1, total), 1)
    row = jnp.zeros((1, total), jnp.int32)
    for r in range(own):
        row = jnp.where(lane == me * own + r, seeds_ref[r], row)
    seed_rows[0] = row
    loads[1].wait()
    loads[2].wait()

    pl.semaphore_wait(barrier, n - 1)

    def spread(phase, count, peer_of, source, target):
        @pl.loop(1, count)
        def _(d):
            peer = peer_of(d)
            pltpu.make_async_remote_copy(
                src_ref=source(peer),
                dst_ref=target(d),
                send_sem=send_sem.at[phase],
                recv_sem=recv_sem.at[phase],
                device_id={"space": peer},
                device_id_type=MESH,
            ).start()

    def anyone(d):
        return lax.rem(me + d, n)

    def in_block(d):
        return base + lax.rem(seat + d, BLOCK)

    def in_group(d):
        return lax.rem(me + BLOCK * d, n)

    def whole(phase, ref):
        return pltpu.make_async_remote_copy(
            src_ref=ref,
            dst_ref=ref,
            send_sem=send_sem.at[phase],
            recv_sem=recv_sem.at[phase],
            device_id={"space": partner},
            device_id_type=MESH,
        )

    def slab_copy(i, source, target, peer):
        return pltpu.make_async_remote_copy(
            src_ref=slabs.at[:, source],
            dst_ref=slabs.at[:, target],
            send_sem=slab_send.at[i],
            recv_sem=slab_recv.at[target],
            device_id={"space": peer},
            device_id_type=MESH,
        )

    def arrived(slot):
        slab_copy(0, slot, slot, partner).wait_recv()

    to_beyond = slab_copy(0, place, BLOCK + 1 - outer, beyond)
    to_mirror = slab_copy(1, place, place, mirror)
    to_partner = slab_copy(2, place, place, partner)

    @pl.when(at_end)
    def _():
        to_beyond.start()

    @pl.when(inside)
    def _():
        to_mirror.start()

    to_partner.start()
    spread(0, n, anyone, lambda peer: seed_rows.at[0], lambda d: seed_rows.at[d])
    spread(1, BLOCK, in_block, lambda peer: weights.at[seat], lambda d: weights.at[seat])

    def lateral(f, shift):
        layers = [
            pltpu.roll(f[s * across : (s + 1) * across], shift % across, 0)
            for s in range(f.shape[0] // across)
        ]
        return jnp.concatenate(layers, axis=0)

    def across_slope(f):
        return (
            lateral(f, 2) - 8.0 * lateral(f, 1) + 8.0 * lateral(f, -1) - lateral(f, -2)
        ) / 12.0

    def along_slope(f):
        width = f.shape[0] - 2 * cells
        g = [
            f[cells + shift * across : cells + width + shift * across] for shift in (-2, -1, 1, 2)
        ]
        return (g[0] - 8.0 * g[1] + 8.0 * g[2] - g[3]) / 12.0

    def keep(q, x):
        high[q * cells : (q + 1) * cells, :], low[q * cells : (q + 1) * cells, :] = split(x)

    for a in range(2):
        f = slabs[a, place]
        keep(a, f)
        keep(4 + a, across_slope(f))
    for load in loads[3:]:
        load.wait()
    table = split(coeff_ref[...])

    seed_bytes = whole(0, seed_rows.at[pl.ds(1, n - 1)])
    seed_bytes.wait_recv()
    seeds = jnp.sum(seed_rows[...], axis=0)
    spot = jnp.broadcast_to(seeds.astype(jnp.float32), (128, total)).T
    spots[...] = spot.reshape(blocks, BLOCK, own, 128)

    def choose(spot):
        spot = jnp.concatenate([spot] * (params // 128), axis=1)
        chosen = spot == lax.broadcasted_iota(jnp.int32, spot.shape, 1).astype(jnp.float32)
        viscosity = jnp.sum(jnp.where(chosen, visc_ref[...], 0.0), axis=1, keepdims=True)
        return chosen.astype(jnp.float32), viscosity

    chosen, viscosity = choose(spot)
    chosen = chosen.astype(jnp.bfloat16)
    now = [product(chosen, half, ROWS).astype(jnp.bfloat16) for half in table]

    def scale_of(held):
        parts = [w[s : s + 1, :] for w in held for s in range(slab)]
        return jnp.concatenate(parts, axis=1) / (cells * n)

    def advance(now, basis, scale, viscosity):
        gathered = product_3(now, basis, LANES)
        size = gathered.shape[1] // 6
        part = [gathered[:, q * size : (q + 1) * size] for q in range(6)]
        fields = [scale * (part[0] * part[2 + a] + part[1] * part[4 + a]) for a in range(2)]
        damped = viscosity * scale
        fields += [damped * part[q] for q in range(2, 6)]
        return product_3(split(jnp.concatenate(fields, axis=1)), basis, ROWS)

    arrived(seat)
    arrived(seat + 2)

    edge_partner = slab_copy(3, outer, outer, partner)
    edge_mirror = slab_copy(4, outer, outer, mirror)
    inner_partner = slab_copy(3, BLOCK - seat, BLOCK - seat, partner)

    @pl.when(at_end)
    def _():
        to_mirror.start()
        edge_partner.start()

    @pl.when(inside)
    def _():
        inner_partner.start()

    for a in range(2):
        f = slabs[a, pl.ds(seat, 3)].reshape(3 * cells, mode_count)
        keep(2 + a, along_slope(f))
    change = advance(now, (high[...], low[...]), scale_of([weights[seat]]), viscosity)
    partial[...] = change.reshape(blocks, BLOCK, own, mode_count)
    spread(
        2,
        BLOCK,
        in_block,
        lambda peer: partial.at[:, peer - base],
        lambda d: landed.at[d - 1],
    )

    @pl.when(at_end)
    def _():
        edge_mirror.start()

    chosen, viscosity = choose(spots[:, seat].reshape(group, 128))
    coeffs = lax.dot(chosen, coeff_ref[...], precision=lax.Precision.HIGHEST)
    forcing = lax.dot(chosen, force_ref[...], precision=lax.Precision.HIGHEST)
    weight_bytes = whole(1, weights.at[pl.ds(0, BLOCK - 1)])
    weight_bytes.wait_recv()
    scale = scale_of([weights[s] for s in range(BLOCK)])

    block_bytes = whole(2, landed)
    block_bytes.wait_recv()
    change = (partial[:, seat] + jnp.sum(landed[...], axis=0)).reshape(group, mode_count)
    group_sum[...] = change
    spread(3, blocks, in_group, lambda peer: group_sum, lambda d: group_landed.at[d - 1])

    other = BLOCK - seat
    late_1 = slab_copy(5, other, other, partner)
    late_2 = slab_copy(6, BLOCK + 1 - outer, BLOCK + 1 - outer, partner)

    @pl.when(at_end)
    def _():
        arrived(other)
        late_1.start()
        arrived(BLOCK + 1 - outer)
        late_2.start()
        arrived(3 - high_end)

    @pl.when(inside)
    def _():
        for k in range(3):
            arrived(lax.rem(seat + 3 + k, BLOCK + 2))

    size = BLOCK * cells

    def keep_wide(q, x):
        wide_high[q * size : (q + 1) * size, :], wide_low[q * size : (q + 1) * size, :] = split(x)

    for a in range(2):
        f = slabs[a].reshape((BLOCK + 2) * cells, mode_count)
        middle = f[cells : cells + size]
        keep_wide(a, middle)
        keep_wide(2 + a, along_slope(f))
        keep_wide(4 + a, across_slope(middle))

    group_bytes = whole(3, group_landed)
    group_bytes.wait_recv()
    change = change + jnp.sum(group_landed[...], axis=0)
    coeffs = coeffs + TIME_STEP * (forcing - change)
    group_coeffs[...] = coeffs.reshape(blocks, own, mode_count)
    group_force[...] = forcing.reshape(blocks, own, mode_count)
    change = advance(split(coeffs), (wide_high[...], wide_low[...]), scale, viscosity)
    last[...] = change.reshape(blocks, own, mode_count)
    spread(
        4, blocks, in_group, lambda peer: last.at[peer // BLOCK], lambda d: last_landed.at[d - 1]
    )
    last_bytes = whole(4, last_landed)
    last_bytes.wait_recv()
    change = last[block] + jnp.sum(last_landed[...], axis=0)
    out_ref[...] = group_coeffs[block] + TIME_STEP * (group_force[block] - change)

    to_mirror.wait_send()
    to_partner.wait_send()

    @pl.when(at_end)
    def _():
        for copy in (to_beyond, edge_partner, edge_mirror, late_1, late_2):
            copy.wait_send()

    @pl.when(inside)
    def _():
        inner_partner.wait_send()

    for sent in (seed_bytes, weight_bytes, block_bytes, group_bytes, last_bytes):
        sent.wait_send()


def shards(modes, cell_weight, seeds, coeff_table, force_table, visc_table):
    components, mode_count, slab_cells, across = modes.shape
    n = lax.axis_size("space")
    blocks = n // BLOCK
    cells = slab_cells * across
    own = seeds.shape[0]
    total = own * n
    params = coeff_table.shape[0]
    f32, bf16 = jnp.float32, jnp.bfloat16
    return pl.pallas_call(
        functools.partial(kernel, n, across),
        out_shape=jax.ShapeDtypeStruct((own, mode_count), f32),
        in_specs=[pl.BlockSpec(memory_space=pl.ANY)] * 6,
        out_specs=pl.BlockSpec(memory_space=pltpu.VMEM),
        scratch_shapes=[
            pltpu.VMEM((components, BLOCK + 2, cells, mode_count), f32),
            pltpu.VMEM((BLOCK, slab_cells, across), f32),
            pltpu.SMEM((own,), jnp.int32),
            pltpu.VMEM((1, params), f32),
            pltpu.VMEM((params, mode_count), f32),
            pltpu.VMEM((params, mode_count), f32),
            pltpu.VMEM((n, 1, total), jnp.int32),
            pltpu.VMEM((blocks, BLOCK, own, 128), f32),
            pltpu.VMEM((6 * cells, mode_count), bf16),
            pltpu.VMEM((6 * cells, mode_count), bf16),
            pltpu.VMEM((6 * BLOCK * cells, mode_count), bf16),
            pltpu.VMEM((6 * BLOCK * cells, mode_count), bf16),
            pltpu.VMEM((blocks, BLOCK, own, mode_count), f32),
            pltpu.VMEM((BLOCK - 1, blocks, own, mode_count), f32),
            pltpu.VMEM((own * blocks, mode_count), f32),
            pltpu.VMEM((blocks - 1, own * blocks, mode_count), f32),
            pltpu.VMEM((blocks, own, mode_count), f32),
            pltpu.VMEM((blocks, own, mode_count), f32),
            pltpu.VMEM((blocks, own, mode_count), f32),
            pltpu.VMEM((blocks - 1, own, mode_count), f32),
            pltpu.SemaphoreType.DMA((6,)),
            pltpu.SemaphoreType.DMA((7,)),
            pltpu.SemaphoreType.DMA((BLOCK + 2,)),
            pltpu.SemaphoreType.DMA((5,)),
            pltpu.SemaphoreType.DMA((5,)),
        ],
        compiler_params=pltpu.CompilerParams(collective_id=0, has_side_effects=True),
    )(
        modes.transpose(0, 2, 3, 1).reshape(components, cells, mode_count),
        cell_weight,
        seeds,
        visc_table.reshape(1, -1),
        coeff_table,
        force_table,
    )


def solution(mesh):
    placed = (
        P("groups", None, "space", None),
        P("space", "groups"),
        P(("groups", "space")),
        P(),
        P(),
        P(),
    )
    return jax.shard_map(
        shards, mesh=mesh, in_specs=placed, out_specs=P(("groups", "space"), None), check_vma=False
    )
```

```python
import functools

import jax
import jax.numpy as jnp
from jax import lax
from jax.experimental import pallas as pl
from jax.experimental.pallas import tpu as pltpu
from jax.sharding import PartitionSpec as P

TIME_STEP = 0.5

MESH = pl.DeviceIdType.MESH

ROWS = ((1,), (0,))
LANES = ((1,), (1,))


def split(x):
    high = x.astype(jnp.bfloat16)
    return high, (x - high.astype(jnp.float32)).astype(jnp.bfloat16)


def product(a, b, contract):
    return lax.dot_general(a, b, (contract, ((), ())), preferred_element_type=jnp.float32)


BLOCK = 4


def product_3(a, b, contract):
    rows = a[0].shape[0]
    both = product(jnp.concatenate(a, axis=0), b[0], contract)
    return (product(a[0], b[1], contract) + both[rows:]) + both[:rows]


def kernel(
    n,
    across,
    modes_hbm,
    weight_hbm,
    seeds_hbm,
    visc_hbm,
    coeff_hbm,
    force_hbm,
    out_ref,
    slabs,
    weights,
    seeds_ref,
    visc_ref,
    coeff_ref,
    force_ref,
    seed_rows,
    spots,
    high,
    low,
    wide_high,
    wide_low,
    partial,
    landed,
    group_sum,
    group_landed,
    group_coeffs,
    group_force,
    last,
    last_landed,
    load_sem,
    slab_send,
    slab_recv,
    send_sem,
    recv_sem,
):
    me = lax.axis_index("space")
    blocks = n // BLOCK
    block, seat = me // BLOCK, lax.rem(me, BLOCK)
    base = me - seat
    own = seeds_hbm.shape[0]
    cells = modes_hbm.shape[1]
    mode_count = modes_hbm.shape[2]
    slab = cells // across
    params = coeff_ref.shape[0]
    total = own * n
    group = own * blocks
    partner = me + 1 - 2 * lax.rem(seat, 2)
    mirror = base + BLOCK - 1 - seat
    place = seat + 1
    high_end = seat // (BLOCK - 1)
    outer = high_end * (BLOCK + 1)
    beyond = lax.rem(me + n - 1 + 2 * high_end, n)
    at_end = (seat == 0) | (seat == BLOCK - 1)
    inside = jnp.logical_not(at_end)

    barrier = pltpu.get_barrier_semaphore()

    @pl.loop(1, n)
    def _(d):
        pl.semaphore_signal(
            barrier, inc=1, device_id={"space": lax.rem(me + d, n)}, device_id_type=MESH
        )

    loads = [
        pltpu.make_async_copy(source, target, load_sem.at[i])
        for i, (source, target) in enumerate(
            (
                (seeds_hbm, seeds_ref),
                (modes_hbm, slabs.at[:, place]),
                (weight_hbm, weights.at[seat]),
                (coeff_hbm, coeff_ref),
                (force_hbm, force_ref),
                (visc_hbm, visc_ref),
            )
        )
    ]
    for load in loads:
        load.start()
    loads[0].wait()
    lane = lax.broadcasted_iota(jnp.int32, (1, total), 1)
    row = jnp.zeros((1, total), jnp.int32)
    for r in range(own):
        row = jnp.where(lane == me * own + r, seeds_ref[r], row)
    seed_rows[0] = row
    loads[1].wait()
    loads[2].wait()

    pl.semaphore_wait(barrier, n - 1)

    def spread(phase, count, peer_of, source, target):
        @pl.loop(1, count)
        def _(d):
            peer = peer_of(d)
            pltpu.make_async_remote_copy(
                src_ref=source(peer),
                dst_ref=target(d),
                send_sem=send_sem.at[phase],
                recv_sem=recv_sem.at[phase],
                device_id={"space": peer},
                device_id_type=MESH,
            ).start()

    def anyone(d):
        return lax.rem(me + d, n)

    def in_block(d):
        return base + lax.rem(seat + d, BLOCK)

    def in_group(d):
        return lax.rem(me + BLOCK * d, n)

    def whole(phase, ref):
        return pltpu.make_async_remote_copy(
            src_ref=ref,
            dst_ref=ref,
            send_sem=send_sem.at[phase],
            recv_sem=recv_sem.at[phase],
            device_id={"space": partner},
            device_id_type=MESH,
        )

    def slab_copy(i, source, target, peer):
        return pltpu.make_async_remote_copy(
            src_ref=slabs.at[:, source],
            dst_ref=slabs.at[:, target],
            send_sem=slab_send.at[i],
            recv_sem=slab_recv.at[target],
            device_id={"space": peer},
            device_id_type=MESH,
        )

    def arrived(slot):
        slab_copy(0, slot, slot, partner).wait_recv()

    to_beyond = slab_copy(0, place, BLOCK + 1 - outer, beyond)
    to_mirror = slab_copy(1, place, place, mirror)
    to_partner = slab_copy(2, place, place, partner)

    spread(0, n, anyone, lambda peer: seed_rows.at[0], lambda d: seed_rows.at[d])

    @pl.when(at_end)
    def _():
        to_beyond.start()

    @pl.when(inside)
    def _():
        to_mirror.start()

    to_partner.start()
    spread(1, BLOCK, in_block, lambda peer: weights.at[seat], lambda d: weights.at[seat])

    def lateral(f, shift):
        layers = [
            pltpu.roll(f[s * across : (s + 1) * across], shift % across, 0)
            for s in range(f.shape[0] // across)
        ]
        return jnp.concatenate(layers, axis=0)

    def across_slope(f):
        return (
            lateral(f, 2) - 8.0 * lateral(f, 1) + 8.0 * lateral(f, -1) - lateral(f, -2)
        ) / 12.0

    def along_slope(f):
        width = f.shape[0] - 2 * cells
        g = [
            f[cells + shift * across : cells + width + shift * across] for shift in (-2, -1, 1, 2)
        ]
        return (g[0] - 8.0 * g[1] + 8.0 * g[2] - g[3]) / 12.0

    def keep(q, x):
        high[q * cells : (q + 1) * cells, :], low[q * cells : (q + 1) * cells, :] = split(x)

    for a in range(2):
        f = slabs[a, place]
        keep(a, f)
        keep(2 + a, across_slope(f))
    for load in loads[3:]:
        load.wait()
    table = split(coeff_ref[...])

    seed_bytes = whole(0, seed_rows.at[pl.ds(1, n - 1)])
    seed_bytes.wait_recv()
    seeds = jnp.sum(seed_rows[...], axis=0)
    spot = jnp.broadcast_to(seeds.astype(jnp.float32), (128, total)).T
    spots[...] = spot.reshape(blocks, BLOCK, own, 128)

    def choose(spot):
        spot = jnp.concatenate([spot] * (params // 128), axis=1)
        chosen = spot == lax.broadcasted_iota(jnp.int32, spot.shape, 1).astype(jnp.float32)
        viscosity = jnp.sum(jnp.where(chosen, visc_ref[...], 0.0), axis=1, keepdims=True)
        return chosen.astype(jnp.float32), viscosity

    chosen, viscosity = choose(spot)
    chosen = chosen.astype(jnp.bfloat16)
    now = [product(chosen, half, ROWS).astype(jnp.bfloat16) for half in table]

    def scale_of(held):
        parts = [w[s : s + 1, :] for w in held for s in range(slab)]
        return jnp.concatenate(parts, axis=1) / (cells * n)

    def pieces(now, high, low, start, count):
        size = high.shape[0] // 6
        rows = slice(start * size, (start + count) * size)
        gathered = product_3(now, (high[rows, :], low[rows, :]), LANES)
        return [gathered[:, q * size : (q + 1) * size] for q in range(count)]

    def advance(part, basis, scale, viscosity):
        fields = [scale * (part[0] * part[4 + a] + part[1] * part[2 + a]) for a in range(2)]
        damped = viscosity * scale
        fields += [damped * part[q] for q in range(2, 6)]
        return product_3(split(jnp.concatenate(fields, axis=1)), basis, ROWS)

    part = pieces(now, high, low, 0, 4)
    arrived(seat)
    arrived(seat + 2)

    edge_partner = slab_copy(3, outer, outer, partner)
    edge_mirror = slab_copy(4, outer, outer, mirror)
    inner_partner = slab_copy(3, BLOCK - seat, BLOCK - seat, partner)

    @pl.when(at_end)
    def _():
        to_mirror.start()
        edge_partner.start()

    @pl.when(inside)
    def _():
        inner_partner.start()

    for a in range(2):
        f = slabs[a, pl.ds(seat, 3)].reshape(3 * cells, mode_count)
        keep(4 + a, along_slope(f))
    part += pieces(now, high, low, 4, 2)
    change = advance(part, (high[...], low[...]), scale_of([weights[seat]]), viscosity)
    partial[...] = change.reshape(blocks, BLOCK, own, mode_count)
    spread(
        2,
        BLOCK,
        in_block,
        lambda peer: partial.at[:, peer - base],
        lambda d: landed.at[d - 1],
    )

    @pl.when(at_end)
    def _():
        edge_mirror.start()

    chosen, viscosity = choose(spots[:, seat].reshape(group, 128))
    coeffs = lax.dot(chosen, coeff_ref[...], precision=lax.Precision.HIGHEST)
    forcing = lax.dot(chosen, force_ref[...], precision=lax.Precision.HIGHEST)
    weight_bytes = whole(1, weights.at[pl.ds(0, BLOCK - 1)])
    weight_bytes.wait_recv()
    scale = scale_of([weights[s] for s in range(BLOCK)])

    block_bytes = whole(2, landed)
    block_bytes.wait_recv()
    change = (partial[:, seat] + jnp.sum(landed[...], axis=0)).reshape(group, mode_count)
    group_sum[...] = change
    spread(3, blocks, in_group, lambda peer: group_sum, lambda d: group_landed.at[d - 1])

    other = BLOCK - seat
    late_1 = slab_copy(5, other, other, partner)
    late_2 = slab_copy(6, BLOCK + 1 - outer, BLOCK + 1 - outer, partner)

    @pl.when(at_end)
    def _():
        arrived(other)
        late_1.start()
        arrived(BLOCK + 1 - outer)
        late_2.start()
        arrived(3 - high_end)

    @pl.when(inside)
    def _():
        for k in range(3):
            arrived(lax.rem(seat + 3 + k, BLOCK + 2))

    size = BLOCK * cells

    def keep_wide(q, x):
        wide_high[q * size : (q + 1) * size, :], wide_low[q * size : (q + 1) * size, :] = split(x)

    for a in range(2):
        f = slabs[a].reshape((BLOCK + 2) * cells, mode_count)
        middle = f[cells : cells + size]
        keep_wide(a, middle)
        keep_wide(2 + a, across_slope(middle))
        keep_wide(4 + a, along_slope(f))

    group_bytes = whole(3, group_landed)
    group_bytes.wait_recv()
    change = change + jnp.sum(group_landed[...], axis=0)
    coeffs = coeffs + TIME_STEP * (forcing - change)
    group_coeffs[...] = coeffs.reshape(blocks, own, mode_count)
    group_force[...] = forcing.reshape(blocks, own, mode_count)
    part = pieces(split(coeffs), wide_high, wide_low, 0, 6)
    change = advance(part, (wide_high[...], wide_low[...]), scale, viscosity)
    last[...] = change.reshape(blocks, own, mode_count)
    spread(
        4, blocks, in_group, lambda peer: last.at[peer // BLOCK], lambda d: last_landed.at[d - 1]
    )
    last_bytes = whole(4, last_landed)
    last_bytes.wait_recv()
    change = last[block] + jnp.sum(last_landed[...], axis=0)
    out_ref[...] = group_coeffs[block] + TIME_STEP * (group_force[block] - change)

    to_mirror.wait_send()
    to_partner.wait_send()

    @pl.when(at_end)
    def _():
        for copy in (to_beyond, edge_partner, edge_mirror, late_1, late_2):
            copy.wait_send()

    @pl.when(inside)
    def _():
        inner_partner.wait_send()

    for sent in (seed_bytes, weight_bytes, block_bytes, group_bytes, last_bytes):
        sent.wait_send()


def shards(modes, cell_weight, seeds, coeff_table, force_table, visc_table):
    components, mode_count, slab_cells, across = modes.shape
    n = lax.axis_size("space")
    blocks = n // BLOCK
    cells = slab_cells * across
    own = seeds.shape[0]
    total = own * n
    params = coeff_table.shape[0]
    f32, bf16 = jnp.float32, jnp.bfloat16
    return pl.pallas_call(
        functools.partial(kernel, n, across),
        out_shape=pltpu.VMEM((own, mode_count), f32),
        in_specs=[pl.BlockSpec(memory_space=pl.ANY)] * 6,
        out_specs=pl.BlockSpec(memory_space=pltpu.VMEM),
        scratch_shapes=[
            pltpu.VMEM((components, BLOCK + 2, cells, mode_count), f32),
            pltpu.VMEM((BLOCK, slab_cells, across), f32),
            pltpu.SMEM((own,), jnp.int32),
            pltpu.VMEM((1, params), f32),
            pltpu.VMEM((params, mode_count), f32),
            pltpu.VMEM((params, mode_count), f32),
            pltpu.VMEM((n, 1, total), jnp.int32),
            pltpu.VMEM((blocks, BLOCK, own, 128), f32),
            pltpu.VMEM((6 * cells, mode_count), bf16),
            pltpu.VMEM((6 * cells, mode_count), bf16),
            pltpu.VMEM((6 * BLOCK * cells, mode_count), bf16),
            pltpu.VMEM((6 * BLOCK * cells, mode_count), bf16),
            pltpu.VMEM((blocks, BLOCK, own, mode_count), f32),
            pltpu.VMEM((BLOCK - 1, blocks, own, mode_count), f32),
            pltpu.VMEM((own * blocks, mode_count), f32),
            pltpu.VMEM((blocks - 1, own * blocks, mode_count), f32),
            pltpu.VMEM((blocks, own, mode_count), f32),
            pltpu.VMEM((blocks, own, mode_count), f32),
            pltpu.VMEM((blocks, own, mode_count), f32),
            pltpu.VMEM((blocks - 1, own, mode_count), f32),
            pltpu.SemaphoreType.DMA((6,)),
            pltpu.SemaphoreType.DMA((7,)),
            pltpu.SemaphoreType.DMA((BLOCK + 2,)),
            pltpu.SemaphoreType.DMA((5,)),
            pltpu.SemaphoreType.DMA((5,)),
        ],
        compiler_params=pltpu.CompilerParams(collective_id=0, has_side_effects=True),
    )(
        modes.transpose(0, 2, 3, 1).reshape(components, cells, mode_count),
        cell_weight,
        seeds,
        visc_table.reshape(1, -1),
        coeff_table,
        force_table,
    )


def solution(mesh):
    placed = (
        P("groups", None, "space", None),
        P("space", "groups"),
        P(("groups", "space")),
        P(),
        P(),
        P(),
    )
    return jax.shard_map(
        shards, mesh=mesh, in_specs=placed, out_specs=P(("groups", "space"), None), check_vma=False
    )
```

```python
import functools

import jax
import jax.numpy as jnp
from jax import lax
from jax.experimental import pallas as pl
from jax.experimental.pallas import tpu as pltpu
from jax.sharding import PartitionSpec as P

TIME_STEP = 0.5

MESH = pl.DeviceIdType.MESH

ROWS = ((1,), (0,))
LANES = ((1,), (1,))


def split(x):
    high = x.astype(jnp.bfloat16)
    return high, (x - high.astype(jnp.float32)).astype(jnp.bfloat16)


def product(a, b, contract):
    return lax.dot_general(a, b, (contract, ((), ())), preferred_element_type=jnp.float32)


BLOCK = 4

HALVES = 2


def product_3(a, b, contract):
    rows = a[0].shape[0]
    both = product(jnp.concatenate(a, axis=0), b[0], contract)
    return (product(a[0], b[1], contract) + both[rows:]) + both[:rows]


def kernel(
    n,
    across,
    modes_hbm,
    weight_hbm,
    seeds_hbm,
    visc_hbm,
    coeff_hbm,
    force_hbm,
    out_ref,
    slabs,
    weights,
    seeds_ref,
    visc_ref,
    coeff_ref,
    force_ref,
    seed_rows,
    spots,
    high,
    low,
    wide_high,
    wide_low,
    partial,
    landed,
    group_sum,
    group_landed,
    group_coeffs,
    group_force,
    last,
    last_landed,
    load_sem,
    slab_send,
    slab_recv,
    send_sem,
    recv_sem,
):
    me = lax.axis_index("space")
    blocks = n // BLOCK
    block, seat = me // BLOCK, lax.rem(me, BLOCK)
    base = me - seat
    own = seeds_hbm.shape[0]
    cells = modes_hbm.shape[1]
    mode_count = modes_hbm.shape[2]
    slab = cells // across
    params = coeff_ref.shape[0]
    total = own * n
    group = own * blocks
    half = blocks // HALVES
    partner = me + 1 - 2 * lax.rem(seat, 2)
    mirror = base + BLOCK - 1 - seat
    place = seat + 1
    high_end = seat // (BLOCK - 1)
    outer = high_end * (BLOCK + 1)
    beyond = lax.rem(me + n - 1 + 2 * high_end, n)
    at_end = (seat == 0) | (seat == BLOCK - 1)
    inside = jnp.logical_not(at_end)

    barrier = pltpu.get_barrier_semaphore()

    @pl.loop(1, n)
    def _(d):
        pl.semaphore_signal(
            barrier, inc=1, device_id={"space": lax.rem(me + d, n)}, device_id_type=MESH
        )

    loads = [
        pltpu.make_async_copy(source, target, load_sem.at[i])
        for i, (source, target) in enumerate(
            (
                (seeds_hbm, seeds_ref),
                (modes_hbm, slabs.at[:, place]),
                (weight_hbm, weights.at[seat]),
                (coeff_hbm, coeff_ref),
                (force_hbm, force_ref),
                (visc_hbm, visc_ref),
            )
        )
    ]
    for load in loads:
        load.start()
    loads[0].wait()
    lane = lax.broadcasted_iota(jnp.int32, (1, total), 1)
    row = jnp.zeros((1, total), jnp.int32)
    for r in range(own):
        row = jnp.where(lane == me * own + r, seeds_ref[r], row)
    seed_rows[0] = row
    loads[1].wait()
    loads[2].wait()

    pl.semaphore_wait(barrier, n - 1)

    def spread(phase, count, peer_of, source, target):
        @pl.loop(1, count)
        def _(d):
            peer = peer_of(d)
            pltpu.make_async_remote_copy(
                src_ref=source(peer),
                dst_ref=target(d),
                send_sem=send_sem.at[phase],
                recv_sem=recv_sem.at[phase],
                device_id={"space": peer},
                device_id_type=MESH,
            ).start()

    def anyone(d):
        return lax.rem(me + d, n)

    def in_block(d):
        return base + lax.rem(seat + d, BLOCK)

    def in_group(d):
        return lax.rem(me + BLOCK * d, n)

    def whole(phase, ref):
        return pltpu.make_async_remote_copy(
            src_ref=ref,
            dst_ref=ref,
            send_sem=send_sem.at[phase],
            recv_sem=recv_sem.at[phase],
            device_id={"space": partner},
            device_id_type=MESH,
        )

    def slab_copy(i, source, target, peer):
        return pltpu.make_async_remote_copy(
            src_ref=slabs.at[:, source],
            dst_ref=slabs.at[:, target],
            send_sem=slab_send.at[i],
            recv_sem=slab_recv.at[target],
            device_id={"space": peer},
            device_id_type=MESH,
        )

    def arrived(slot):
        slab_copy(0, slot, slot, partner).wait_recv()

    to_beyond = slab_copy(0, place, BLOCK + 1 - outer, beyond)
    to_mirror = slab_copy(1, place, place, mirror)
    to_partner = slab_copy(2, place, place, partner)

    spread(0, n, anyone, lambda peer: seed_rows.at[0], lambda d: seed_rows.at[d])

    @pl.when(at_end)
    def _():
        to_beyond.start()

    @pl.when(inside)
    def _():
        to_mirror.start()

    to_partner.start()
    spread(1, BLOCK, in_block, lambda peer: weights.at[seat], lambda d: weights.at[seat])

    def lateral(f, shift):
        layers = [
            pltpu.roll(f[s * across : (s + 1) * across], shift % across, 0)
            for s in range(f.shape[0] // across)
        ]
        return jnp.concatenate(layers, axis=0)

    def across_slope(f):
        return (
            lateral(f, 2) - 8.0 * lateral(f, 1) + 8.0 * lateral(f, -1) - lateral(f, -2)
        ) / 12.0

    def along_slope(f):
        width = f.shape[0] - 2 * cells
        g = [
            f[cells + shift * across : cells + width + shift * across] for shift in (-2, -1, 1, 2)
        ]
        return (g[0] - 8.0 * g[1] + 8.0 * g[2] - g[3]) / 12.0

    def keep(q, x):
        high[q * cells : (q + 1) * cells, :], low[q * cells : (q + 1) * cells, :] = split(x)

    for a in range(2):
        f = slabs[a, place]
        keep(a, f)
        keep(2 + a, across_slope(f))
    for load in loads[3:]:
        load.wait()
    table = split(coeff_ref[...])

    seed_bytes = whole(0, seed_rows.at[pl.ds(1, n - 1)])
    seed_bytes.wait_recv()
    seeds = jnp.sum(seed_rows[...], axis=0)
    spot = jnp.broadcast_to(seeds.astype(jnp.float32), (128, total)).T
    spots[...] = spot.reshape(blocks, BLOCK, own, 128)

    def choose(spot):
        spot = jnp.concatenate([spot] * (params // 128), axis=1)
        chosen = spot == lax.broadcasted_iota(jnp.int32, spot.shape, 1).astype(jnp.float32)
        viscosity = jnp.sum(jnp.where(chosen, visc_ref[...], 0.0), axis=1, keepdims=True)
        return chosen.astype(jnp.float32), viscosity

    chosen, viscosity = choose(spot)
    chosen = chosen.astype(jnp.bfloat16)
    now = [product(chosen, half, ROWS).astype(jnp.bfloat16) for half in table]

    def scale_of(held):
        parts = [w[s : s + 1, :] for w in held for s in range(slab)]
        return jnp.concatenate(parts, axis=1) / (cells * n)

    def pieces(now, high, low, start, count):
        size = high.shape[0] // 6
        rows = slice(start * size, (start + count) * size)
        gathered = product_3(now, (high[rows, :], low[rows, :]), LANES)
        return [gathered[:, q * size : (q + 1) * size] for q in range(count)]

    def advance(part, basis, scale, viscosity):
        fields = [scale * (part[0] * part[4 + a] + part[1] * part[2 + a]) for a in range(2)]
        damped = viscosity * scale
        fields += [damped * part[q] for q in range(2, 6)]
        return product_3(split(jnp.concatenate(fields, axis=1)), basis, ROWS)

    part = pieces(now, high, low, 0, 4)
    arrived(seat)
    arrived(seat + 2)

    edge_partner = slab_copy(3, outer, outer, partner)
    edge_mirror = slab_copy(4, outer, outer, mirror)
    inner_partner = slab_copy(3, BLOCK - seat, BLOCK - seat, partner)

    @pl.when(at_end)
    def _():
        to_mirror.start()
        edge_partner.start()

    @pl.when(inside)
    def _():
        inner_partner.start()

    for a in range(2):
        f = slabs[a, pl.ds(seat, 3)].reshape(3 * cells, mode_count)
        keep(4 + a, along_slope(f))
    part += pieces(now, high, low, 4, 2)
    near_scale = scale_of([weights[seat]])
    for h in range(HALVES):
        rows = slice(h * total // HALVES, (h + 1) * total // HALVES)
        change = advance(
            [p[rows] for p in part], (high[...], low[...]), near_scale, viscosity[rows]
        )
        partial[h * half : (h + 1) * half] = change.reshape(half, BLOCK, own, mode_count)
        spread(
            2 + h,
            BLOCK,
            in_block,
            lambda peer: partial.at[pl.ds(h * half, half), peer - base],
            lambda d: landed.at[h, d - 1],
        )

    @pl.when(at_end)
    def _():
        edge_mirror.start()

    chosen, viscosity = choose(spots[:, seat].reshape(group, 128))
    coeffs = lax.dot(chosen, coeff_ref[...], precision=lax.Precision.HIGHEST)
    forcing = lax.dot(chosen, force_ref[...], precision=lax.Precision.HIGHEST)
    weight_bytes = whole(1, weights.at[pl.ds(0, BLOCK - 1)])
    weight_bytes.wait_recv()
    scale = scale_of([weights[s] for s in range(BLOCK)])

    sums, block_bytes, group_bytes = [], [], []
    for h in range(HALVES):
        block_bytes.append(whole(2 + h, landed.at[h]))
        block_bytes[h].wait_recv()
        summed = partial[h * half : (h + 1) * half, seat] + jnp.sum(landed[h], axis=0)
        sums.append(summed.reshape(own * half, mode_count))
        group_sum[h] = sums[h]
        spread(
            2 + HALVES + h,
            blocks,
            in_group,
            lambda peer: group_sum.at[h],
            lambda d: group_landed.at[h, d - 1],
        )

    other = BLOCK - seat
    late_1 = slab_copy(5, other, other, partner)
    late_2 = slab_copy(6, BLOCK + 1 - outer, BLOCK + 1 - outer, partner)

    @pl.when(at_end)
    def _():
        arrived(other)
        late_1.start()
        arrived(BLOCK + 1 - outer)
        late_2.start()
        arrived(3 - high_end)

    @pl.when(inside)
    def _():
        for k in range(3):
            arrived(lax.rem(seat + 3 + k, BLOCK + 2))

    size = BLOCK * cells

    def keep_wide(q, x):
        wide_high[q * size : (q + 1) * size, :], wide_low[q * size : (q + 1) * size, :] = split(x)

    for a in range(2):
        f = slabs[a].reshape((BLOCK + 2) * cells, mode_count)
        middle = f[cells : cells + size]
        keep_wide(a, middle)
        keep_wide(2 + a, across_slope(middle))
        keep_wide(4 + a, along_slope(f))

    for h in range(HALVES):
        group_bytes.append(whole(2 + HALVES + h, group_landed.at[h]))
        group_bytes[h].wait_recv()
        sums[h] = sums[h] + jnp.sum(group_landed[h], axis=0)
    change = jnp.concatenate(sums, axis=0)
    coeffs = coeffs + TIME_STEP * (forcing - change)
    group_coeffs[...] = coeffs.reshape(blocks, own, mode_count)
    group_force[...] = forcing.reshape(blocks, own, mode_count)
    part = pieces(split(coeffs), wide_high, wide_low, 0, 6)
    change = advance(part, (wide_high[...], wide_low[...]), scale, viscosity)
    last[...] = change.reshape(blocks, own, mode_count)
    spread(
        2 + 2 * HALVES, blocks, in_group, lambda peer: last.at[peer // BLOCK], lambda d: last_landed.at[d - 1]
    )
    last_bytes = whole(2 + 2 * HALVES, last_landed)
    last_bytes.wait_recv()
    change = last[block] + jnp.sum(last_landed[...], axis=0)
    out_ref[...] = group_coeffs[block] + TIME_STEP * (group_force[block] - change)

    to_mirror.wait_send()
    to_partner.wait_send()

    @pl.when(at_end)
    def _():
        for copy in (to_beyond, edge_partner, edge_mirror, late_1, late_2):
            copy.wait_send()

    @pl.when(inside)
    def _():
        inner_partner.wait_send()

    for sent in (seed_bytes, weight_bytes, *block_bytes, *group_bytes, last_bytes):
        sent.wait_send()


def shards(modes, cell_weight, seeds, coeff_table, force_table, visc_table):
    components, mode_count, slab_cells, across = modes.shape
    n = lax.axis_size("space")
    blocks = n // BLOCK
    cells = slab_cells * across
    own = seeds.shape[0]
    total = own * n
    params = coeff_table.shape[0]
    f32, bf16 = jnp.float32, jnp.bfloat16
    return pl.pallas_call(
        functools.partial(kernel, n, across),
        out_shape=pltpu.VMEM((own, mode_count), f32),
        in_specs=[pl.BlockSpec(memory_space=pl.ANY)] * 6,
        out_specs=pl.BlockSpec(memory_space=pltpu.VMEM),
        scratch_shapes=[
            pltpu.VMEM((components, BLOCK + 2, cells, mode_count), f32),
            pltpu.VMEM((BLOCK, slab_cells, across), f32),
            pltpu.SMEM((own,), jnp.int32),
            pltpu.VMEM((1, params), f32),
            pltpu.VMEM((params, mode_count), f32),
            pltpu.VMEM((params, mode_count), f32),
            pltpu.VMEM((n, 1, total), jnp.int32),
            pltpu.VMEM((blocks, BLOCK, own, 128), f32),
            pltpu.VMEM((6 * cells, mode_count), bf16),
            pltpu.VMEM((6 * cells, mode_count), bf16),
            pltpu.VMEM((6 * BLOCK * cells, mode_count), bf16),
            pltpu.VMEM((6 * BLOCK * cells, mode_count), bf16),
            pltpu.VMEM((blocks, BLOCK, own, mode_count), f32),
            pltpu.VMEM((HALVES, BLOCK - 1, blocks // HALVES, own, mode_count), f32),
            pltpu.VMEM((HALVES, own * blocks // HALVES, mode_count), f32),
            pltpu.VMEM((HALVES, blocks - 1, own * blocks // HALVES, mode_count), f32),
            pltpu.VMEM((blocks, own, mode_count), f32),
            pltpu.VMEM((blocks, own, mode_count), f32),
            pltpu.VMEM((blocks, own, mode_count), f32),
            pltpu.VMEM((blocks - 1, own, mode_count), f32),
            pltpu.SemaphoreType.DMA((6,)),
            pltpu.SemaphoreType.DMA((7,)),
            pltpu.SemaphoreType.DMA((BLOCK + 2,)),
            pltpu.SemaphoreType.DMA((3 + 2 * HALVES,)),
            pltpu.SemaphoreType.DMA((3 + 2 * HALVES,)),
        ],
        compiler_params=pltpu.CompilerParams(collective_id=0, has_side_effects=True),
    )(
        modes.transpose(0, 2, 3, 1).reshape(components, cells, mode_count),
        cell_weight,
        seeds,
        visc_table.reshape(1, -1),
        coeff_table,
        force_table,
    )


def solution(mesh):
    placed = (
        P("groups", None, "space", None),
        P("space", "groups"),
        P(("groups", "space")),
        P(),
        P(),
        P(),
    )
    return jax.shard_map(
        shards, mesh=mesh, in_specs=placed, out_specs=P(("groups", "space"), None), check_vma=False
    )
```
